512 devices in a mesh: prompt: 32 (over y, z_hi, core), sample: 16 (over z_lo, x).
Axes of the slice: x: 4, y: 4, z: 16 (z_hi: 4, z_lo: 4; z = z_hi * 4 + z_lo), core: 2. Of those that a mesh axis runs over, the one named last changes fastest.
Arguments:
- queries: bfloat16 [32, 8192, 1792], P('prompt', 'sample'), may hold values from -60 to 60
- prompt_keys: bfloat16 [32, 1024, 256], P('prompt', 'sample'), may hold values from -4 to 4
- prompt_value_rows: bfloat16 [32, 1024, 256], P('prompt', 'sample'), may hold values from -4 to 4
- reply_keys: bfloat16 [32, 8192, 256], P('prompt', 'sample'), may hold values from -4 to 4
- response_values: bfloat16 [32, 8192, 256], P('prompt', 'sample'), may hold values from -4 to 4
- lengths: int32 [32, 16], P('prompt'), may hold values from 1 to 4, as said below
- hand_counts: int32 [32, 16, 2], P('prompt'), may hold values from 0 to 2, as said below
Outputs:
- attended: bfloat16 [32, 8192, 1792], P('prompt', 'sample')
The draws below stay inside these ranges and needn't reach their ends.
Inputs may be any that keep to these rules, and one draw needn't show every extreme that they name: lengths[p, s] counts the live tiles of response s; some response of every prompt has 4 tiles. hand_counts[p, s, k] is the number of tiles that device s hands to its section-k partner; of two partners at most one hands tiles, and every load stays between 1 and 4.
All inputs are finite; a program needn't handle non-finite values.
Results may differ from the reference program's by a relative error of at most 0.0038.
Values may be sent and summed in bfloat16 or wider, within the bound.
A program may use at most 64 MiB of HBM per device.

```python
import math
import jax
import jax.numpy as jnp
from jax import lax

HQ = 14
KEY_VALUE_HEADS = 2
QUERY_PER_KEY = 7
HEAD_WIDTH = 128
TILE_TOKENS = 128
MOST_TILES = 4
SECTIONS = 2
PROMPT_LENGTH = 1024
PROMPT_COUNT = 32
RESPONSE_ROWS = 8192
N_SAMPLE = 16


def random_source(key, dims, spread, limit):
    return jnp.clip(jax.random.normal(key, dims, jnp.float32) * spread, -limit, limit)


def key_fields(key):
    prefix_tokens = random_source(jax.random.fold_in(key, 11), (PROMPT_COUNT, PROMPT_LENGTH, KEY_VALUE_HEADS * HEAD_WIDTH), 1.0, 4.0)
    answer_output = random_source(jax.random.fold_in(key, 12), (PROMPT_COUNT, N_SAMPLE * MOST_TILES * TILE_TOKENS, KEY_VALUE_HEADS * HEAD_WIDTH), 1.0, 4.0)
    return (prefix_tokens, answer_output)


def draw_queries(key, part):
    base_field = random_source(jax.random.fold_in(key, 13), (PROMPT_COUNT, N_SAMPLE * MOST_TILES * TILE_TOKENS, HQ * HEAD_WIDTH), 2.0, 12.0)
    return base_field.astype(jnp.bfloat16)


def draw_prompt_keys(key, part):
    return key_fields(key)[0].astype(jnp.bfloat16)


def draw_reply_keys(key, part):
    return key_fields(key)[1].astype(jnp.bfloat16)


def balance_plan(key):
    source_key = jax.random.fold_in(key, 7)
    first_draw = jax.random.randint(jax.random.fold_in(source_key, 1), (PROMPT_COUNT, N_SAMPLE), 1, MOST_TILES + 1)
    second_draw = jax.random.randint(jax.random.fold_in(source_key, 2), (PROMPT_COUNT, N_SAMPLE), 1, MOST_TILES + 1)
    length_table = jnp.minimum(first_draw, second_draw).astype(jnp.int32)
    length_table = length_table.at[:, 0].set(MOST_TILES).at[:, N_SAMPLE // 2].set(1)
    coins = jax.random.randint(jax.random.fold_in(source_key, 3), (PROMPT_COUNT, SECTIONS, N_SAMPLE), 0, 2).astype(jnp.int32)
    coins = coins.at[:, 0, 0].set(1)
    devices = jnp.arange(N_SAMPLE, dtype=jnp.int32)
    top_bit = N_SAMPLE.bit_length() - 1
    burden = length_table
    handed = []
    for section_index in range(SECTIONS):
        partner = devices ^ 1 << top_bit - 1 - section_index
        lower = jnp.minimum(devices, partner)
        rounding = coins[:, section_index][:, lower]
        spread_now = burden - burden[:, partner]
        giving = jnp.where(spread_now > 0, (spread_now + rounding) // 2, 0).astype(jnp.int32)
        handed.append(giving)
        burden = burden - giving + giving[:, partner]
    return (length_table, jnp.stack(handed, axis=-1))


def draw_lengths(key, part):
    return balance_plan(key)[0]


def draw_hand_counts(key, part):
    return balance_plan(key)[1]


def block_scale(own_key, extent, cuts, least, largest):
    def one(axis_at, shards_of):
        heights = jax.random.uniform(jax.random.fold_in(jax.random.fold_in(own_key, 6), axis_at), (shards_of,), jnp.float32, least / len(cuts), largest / len(cuts))
        return jnp.repeat(jnp.exp(heights), extent[axis_at] // shards_of).reshape((-1,) + (1,) * (len(extent) - axis_at - 1))

    loudness = one(*cuts[0])
    for cut in cuts[1:]:
        loudness = loudness * one(*cut)
    return loudness


def noise(rng, extent, width, most, split=(), kind=jnp.bfloat16):
    entries = jax.random.normal(rng, extent, jnp.float32) * width
    if len(split) > 0:
        entries = block_scale(rng, extent, split, -0.22, 0.18) * entries
    return jnp.clip(entries, min=-most, max=most).astype(kind)


def setup_inputs(seed: int = 0) -> dict:
    streams_of = jax.random.split(jax.random.key(seed), 8)
    queries = draw_queries(jax.random.fold_in(streams_of[7], 71), 0)
    prompt_keys = draw_prompt_keys(jax.random.fold_in(streams_of[7], 71), 0)
    prompt_value_rows = noise(streams_of[2], (PROMPT_COUNT, PROMPT_LENGTH, KEY_VALUE_HEADS * HEAD_WIDTH), 1.0, 4.0, ((0, 32), (1, 16)))
    reply_keys = draw_reply_keys(jax.random.fold_in(streams_of[7], 71), 0)
    response_values = noise(streams_of[4], (PROMPT_COUNT, RESPONSE_ROWS, KEY_VALUE_HEADS * HEAD_WIDTH), 1.0, 4.0, ((0, 32), (1, 16)))
    lengths = draw_lengths(jax.random.fold_in(streams_of[7], 71), 0)
    hand_counts = draw_hand_counts(jax.random.fold_in(streams_of[7], 71), 0)
    return {"queries": queries, "prompt_keys": prompt_keys, "prompt_value_rows": prompt_value_rows, "reply_keys": reply_keys, "response_values": response_values, "lengths": lengths, "hand_counts": hand_counts}


def attend(query_tile_rows, key_row_block, value_row_block, allowed):
    query_head_block = query_tile_rows.astype(jnp.float32).reshape(TILE_TOKENS, KEY_VALUE_HEADS, QUERY_PER_KEY, HEAD_WIDTH)
    key_head_block = key_row_block.astype(jnp.float32).reshape(-1, KEY_VALUE_HEADS, HEAD_WIDTH)
    value_head_block = value_row_block.astype(jnp.float32).reshape(-1, KEY_VALUE_HEADS, HEAD_WIDTH)
    scores = jnp.einsum('tkgd,skd->kgts', query_head_block, key_head_block) * (1.0 / math.sqrt(HEAD_WIDTH))
    if allowed is not None:
        scores = jnp.where(allowed, scores, -1e+30)
    maxima = lax.optimization_barrier(jnp.max(scores, axis=-1, keepdims=True))
    exponent = jnp.exp(scores - maxima)
    totals = lax.optimization_barrier(jnp.sum(exponent, axis=-1, keepdims=True))
    weights = lax.optimization_barrier(exponent.astype(jnp.bfloat16)).astype(jnp.float32)
    blended_output = jnp.einsum('kgts,skd->tkgd', weights, value_head_block) / jnp.transpose(totals, (2, 0, 1, 3))
    levels = maxima[..., 0] + jnp.log(totals[..., 0])
    return (blended_output, levels)

def combine(first_mix, first_level, second_mix, second_level):
    ceiling = jnp.maximum(first_level, second_level)
    first_weight = jnp.transpose(jnp.exp(first_level - ceiling), (2, 0, 1))[..., None]
    second_weight = jnp.transpose(jnp.exp(second_level - ceiling), (2, 0, 1))[..., None]
    blended_output = (first_weight * first_mix + second_weight * second_mix) / (first_weight + second_weight)
    return blended_output.reshape(TILE_TOKENS, KEY_VALUE_HEADS * QUERY_PER_KEY * HEAD_WIDTH).astype(jnp.bfloat16)

def settle(length_row, hand_rows):
    devices = jnp.arange(N_SAMPLE, dtype=jnp.int32)
    slot_ids = jnp.arange(MOST_TILES, dtype=jnp.int32)
    slot_table = jnp.where(slot_ids[None, :] < length_row[:, None], devices[:, None] * MOST_TILES + slot_ids[None, :], -1)
    burden = length_row
    top_bit = N_SAMPLE.bit_length() - 1
    for section_index in range(SECTIONS):
        partner = devices ^ 1 << top_bit - 1 - section_index
        giving = hand_rows[:, section_index]
        getting = giving[partner]
        keeping = burden - giving
        offset = slot_ids[None, :] - keeping[:, None]
        source = jnp.clip(burden[partner][:, None] - getting[:, None] + offset, 0, MOST_TILES - 1)
        incoming = jnp.take_along_axis(slot_table[partner], source, axis=1)
        slot_table = jnp.where(offset < 0, slot_table, jnp.where(offset < getting[:, None], incoming, -1))
        burden = keeping + getting
    return slot_table

def reference(queries, prompt_keys, prompt_value_rows, reply_keys, response_values, lengths, hand_counts):

    def one_prompt(pieces):
        query_rows, key_prompt, value_prompt, key_reply, value_reply, length_row, hand_rows = pieces
        query_tiles = query_rows.reshape(N_SAMPLE * MOST_TILES, TILE_TOKENS, -1)
        offsets = jnp.arange(TILE_TOKENS, dtype=jnp.int32)
        positions = jnp.arange(MOST_TILES * TILE_TOKENS, dtype=jnp.int32)

        def one_tile(number):
            sample = number // MOST_TILES
            within = number % MOST_TILES
            query_tile_rows = query_tiles[number]
            first_row = (sample * MOST_TILES * TILE_TOKENS).astype(jnp.int32)
            own_keys = lax.dynamic_slice_in_dim(key_reply, first_row, MOST_TILES * TILE_TOKENS, 0)
            own_values = lax.dynamic_slice_in_dim(value_reply, first_row, MOST_TILES * TILE_TOKENS, 0)
            allowed = positions[None, :] <= (within * TILE_TOKENS + offsets)[:, None]
            reply_mix, reply_level = attend(query_tile_rows, own_keys, own_values, allowed)
            reply_mix = lax.optimization_barrier(reply_mix.astype(jnp.bfloat16)).astype(jnp.float32)
            prompt_mix, prompt_level = attend(query_tile_rows, key_prompt, value_prompt, None)
            result = combine(prompt_mix, prompt_level, reply_mix, reply_level)
            is_live = within < length_row[sample]
            return jnp.where(is_live, result, jnp.zeros_like(result))
        results = lax.map(one_tile, jnp.arange(N_SAMPLE * MOST_TILES, dtype=jnp.int32))
        slot_table = settle(length_row, hand_rows)
        placed = results[jnp.clip(slot_table, 0, N_SAMPLE * MOST_TILES - 1)]
        placed = jnp.where((slot_table >= 0)[:, :, None, None], placed, jnp.zeros_like(placed))
        return placed.reshape(N_SAMPLE * MOST_TILES * TILE_TOKENS, -1)
    return lax.map(one_prompt, (queries, prompt_keys, prompt_value_rows, reply_keys, response_values, lengths, hand_counts))
```

```python
import functools
import math

import jax
import jax.numpy as jnp
from jax import lax
from jax.experimental import pallas as pl
from jax.experimental.pallas import tpu as pltpu
from jax.sharding import PartitionSpec as P

KEY_VALUE_HEADS = 2
QUERY_PER_KEY = 7
HEADS = KEY_VALUE_HEADS * QUERY_PER_KEY
HEAD_WIDTH = 128
TILE_TOKENS = 128
MOST_TILES = 4
ALONG_X = 4
ALONG_Z = 4
LAG_SECOND = 2
LAG_OUT = 4

LOG_SCALE = math.log2(math.e) / math.sqrt(HEAD_WIDTH)


def dot_nt(a, b):
    return lax.dot_general(a, b, (((1,), (1,)), ((), ())), preferred_element_type=jnp.float32)


def softmax_parts(scores):
    top = jnp.max(scores, axis=-1, keepdims=True)
    weights = jnp.exp2((scores - top) * LOG_SCALE)
    total = jnp.sum(weights, axis=-1, keepdims=True)
    return top, weights.astype(jnp.bfloat16), total


def weigh(weights, values):
    return jnp.dot(weights, values, preferred_element_type=jnp.float32)


def reply_part(query, keys, values, half):
    rows = 2 * TILE_TOKENS
    seen = (half + 1) * rows
    scores = dot_nt(query, keys[:seen])
    row = lax.broadcasted_iota(jnp.int32, (rows, rows), 0)
    col = lax.broadcasted_iota(jnp.int32, (rows, rows), 1)
    last = jnp.where(col <= row, scores[:, half * rows :], -1e30)
    if half:
        last = jnp.concatenate([scores[:, : half * rows], last], axis=1)
    top, weights, total = softmax_parts(last)
    return top, total, weigh(weights, values[:seen])


def combine(p_top, p_total, p_mix, r_top, r_total, r_mix):
    top = jnp.maximum(p_top, r_top)
    a = jnp.exp2((p_top - top) * LOG_SCALE)
    b = jnp.exp2((r_top - top) * LOG_SCALE)
    inverse = 1.0 / (a * p_total + b * r_total)
    return (p_mix * (a * inverse) + r_mix * (b * inverse)).astype(jnp.bfloat16)


def kernel(
    q_hbm, pk_hbm, pv_hbm, rk_hbm, rv_hbm, len_ref, hand_ref, out_hbm,
    q_buf, kv, rkv, own, send1, recv1, send2, recv2, out_buf,
    in_sem, own_sem, z_send, z_recv, x_send, x_recv, d_send, d_recv,
    s1_sem, r1_sem, s2_sem, r2_sem, out_sem,
):
    me = lax.axis_index("sample")
    z = me // ALONG_X
    x = me % ALONG_X

    def at(zz, xx):
        return {"sample": zz * ALONG_X + xx}

    z_peers = [at((z + d) % ALONG_Z, x) for d in (1, 2, 3)]
    right = at(z, (x + 1) % ALONG_X)
    left = at(z, (x + 3) % ALONG_X)
    first_partner = z_peers[1]
    second_partner = at(z + 1 - 2 * (z % 2), x)
    MESH = pl.DeviceIdType.MESH

    barrier = pltpu.get_barrier_semaphore()
    for peer in z_peers + [right, left]:
        pl.semaphore_signal(barrier, inc=1, device_id=peer, device_id_type=MESH)

    width = HEAD_WIDTH
    own_rows = pl.ds(pl.multiple_of(x * 256 + z * 64, 64), 64)
    prompt_side = (pk_hbm, pv_hbm)
    reply_side = (rk_hbm, rv_hbm)
    own_copies = [
        pltpu.make_async_copy(
            prompt_side[kind].at[:, g * width : (g + 1) * width],
            kv.at[g, kind, own_rows, :],
            own_sem.at[g, kind],
        )
        for g in range(2)
        for kind in range(2)
    ]
    in_copies = [pltpu.make_async_copy(q_hbm, q_buf, in_sem.at[0])] + [
        pltpu.make_async_copy(
            reply_side[kind].at[:, g * width : (g + 1) * width],
            rkv.at[g, kind],
            in_sem.at[1 + 2 * g + kind],
        )
        for g in range(2)
        for kind in range(2)
    ]
    for copy in own_copies + in_copies:
        copy.start()

    def partner_of(mask_z):
        return ((z + 2) % 4 if mask_z == 2 else z + 1 - 2 * (z % 2)) * ALONG_X + x

    give1 = hand_ref[0, 0, me]
    get1 = hand_ref[0, 0, partner_of(2)]
    give2 = hand_ref[0, 1, me]
    get2 = hand_ref[0, 1, partner_of(1)]
    keep1 = len_ref[0, me] - give1
    keep2 = keep1 + get1 - give2
    load2 = keep2 + get2

    def z_copy(g, kind, d):
        return pltpu.make_async_remote_copy(
            prompt_side[kind].at[:, g * width : (g + 1) * width],
            kv.at[g, kind, own_rows, :],
            z_send.at[g, kind, d],
            z_recv.at[g, kind, d],
            device_id=z_peers[d],
            device_id_type=MESH,
        )

    def column(g, xx):
        return kv.at[g, :, pl.ds(pl.multiple_of(xx * 256, 256), 256), :]

    def half_column(g, kind, xx):
        return kv.at[g, kind, pl.ds(pl.multiple_of(xx * 256, 256), 256), :]

    def x_copy(g, way):
        return pltpu.make_async_remote_copy(
            column(g, x), column(g, x), x_send.at[g, way], x_recv.at[g, way],
            device_id=(right, left)[way], device_id_type=MESH,
        )

    def d_copy(g, way):
        source = ((x + 3) % ALONG_X, (x + 1) % ALONG_X)[way]
        return pltpu.make_async_remote_copy(
            half_column(g, way, source), half_column(g, way, source),
            d_send.at[g, way], d_recv.at[g, way],
            device_id=(right, left)[way], device_id_type=MESH,
        )

    pl.semaphore_wait(barrier, 5)
    for g in range(2):
        for d in (1, 0, 2):
            for kind in range(2):
                z_copy(g, kind, d).start()
    for copy in own_copies:
        copy.wait()
    for g in range(2):
        for d in range(3):
            for kind in range(2):
                z_copy(g, kind, d).wait_recv()
        for way in range(2):
            x_copy(g, way).start()
    for copy in in_copies:
        copy.wait()

    def forward_diagonal(g):
        for way in range(2):
            x_copy(g, way).wait_recv()
            d_copy(g, way).start()

    def gathered(g):
        for way in range(2):
            d_copy(g, way).wait_recv()

    forward_diagonal(0)

    def s1_copy(c):
        return pltpu.make_async_remote_copy(
            send1.at[c], recv1.at[c], s1_sem.at[c], r1_sem.at[c],
            device_id=first_partner, device_id_type=MESH,
        )

    def s2_copy(c):
        return pltpu.make_async_remote_copy(
            send2.at[c], recv2.at[c], s2_sem.at[c], r2_sem.at[c],
            device_id=second_partner, device_id_type=MESH,
        )

    def out_copy(c):
        return pltpu.make_async_copy(
            out_buf.at[c],
            out_hbm.at[:, :, pl.ds(pl.multiple_of(c * width, width), width)],
            out_sem.at[c],
        )

    def top_two(keep, one, two, three):
        first = jnp.where(keep == 1, one, jnp.where(keep == 2, two, three))
        return first, jnp.where(keep == 1, two, three)

    def placed(keep, one, two, three, a, b):
        return (
            jnp.where(keep == 1, a, one),
            jnp.where(keep == 1, b, jnp.where(keep == 2, a, two)),
            jnp.where(keep == 2, b, jnp.where(keep == 3, a, three)),
        )

    def attend(c):
        g = c // QUERY_PER_KEY
        cols = pl.ds(pl.multiple_of(c * width, width), width)
        rows = 2 * TILE_TOKENS
        reply = [
            reply_part(q_buf[h * rows : (h + 1) * rows, cols], rkv.at[g, 0], rkv.at[g, 1], h)
            for h in range(2)
        ]

        @pl.when(c == 0)
        def _():
            gathered(0)

        @pl.when(c == QUERY_PER_KEY)
        def _():
            gathered(1)

        tiles = []
        for h in range(2):
            scores = dot_nt(q_buf[h * rows : (h + 1) * rows, cols], kv[g, 0])
            top, weights, total = softmax_parts(scores)
            mix = weigh(weights, kv[g, 1])
            r_top, r_total, r_mix = reply[h]
            result = combine(top, total, mix, r_top, r_total, r_mix)
            tiles += [result[:TILE_TOKENS], result[TILE_TOKENS:]]
        for t in range(MOST_TILES):
            own[c, t] = tiles[t]
        first, second = top_two(keep1, tiles[1], tiles[2], tiles[3])
        send1[c, 0] = first
        send1[c, 1] = second

    def step(c, _):
        @pl.when(c < HEADS)
        def _():
            attend(c)
            s1_copy(c).start()

        @pl.when(c == 0)
        def _():
            forward_diagonal(1)

        @pl.when((c >= LAG_SECOND) & (c < HEADS + LAG_SECOND))
        def _():
            d = c - LAG_SECOND
            s1_copy(d).wait_recv()
            slots = placed(keep1, own[d, 1], own[d, 2], own[d, 3], recv1[d, 0], recv1[d, 1])
            first, second = top_two(keep2, *slots)
            send2[d, 0] = first
            send2[d, 1] = second
            s2_copy(d).start()
            for t in range(3):
                own[d, t + 1] = slots[t]

        @pl.when(c >= LAG_OUT)
        def _():
            e = c - LAG_OUT
            s2_copy(e).wait_recv()
            slots = placed(keep2, own[e, 1], own[e, 2], own[e, 3], recv2[e, 0], recv2[e, 1])
            out_buf[e, 0] = own[e, 0]
            for t in range(3):
                out_buf[e, t + 1] = jnp.where(t + 1 < load2, slots[t], jnp.zeros_like(slots[t]))
            out_copy(e).start()

        return 0

    lax.fori_loop(0, HEADS + LAG_OUT, step, 0)

    for g in range(2):
        for d in range(3):
            for kind in range(2):
                z_copy(g, kind, d).wait_send()
        for way in range(2):
            x_copy(g, way).wait_send()
            d_copy(g, way).wait_send()

    def finish(c, _):
        s1_copy(c).wait_send()
        s2_copy(c).wait_send()
        out_copy(c).wait()
        return 0

    lax.fori_loop(0, HEADS, finish, 0)


def per_device(
    queries, prompt_keys, prompt_value_rows, reply_keys, response_values, lengths, hand_counts
):
    half = jnp.bfloat16
    pair = (HEADS, 2, TILE_TOKENS, HEAD_WIDTH)
    four = (HEADS, MOST_TILES, TILE_TOKENS, HEAD_WIDTH)
    dma = pltpu.SemaphoreType.DMA
    anywhere = pl.BlockSpec(memory_space=pl.ANY)
    scalars = pl.BlockSpec(memory_space=pltpu.SMEM)
    out = pl.pallas_call(
        kernel,
        out_shape=jax.ShapeDtypeStruct((MOST_TILES, TILE_TOKENS, HEADS * HEAD_WIDTH), half),
        in_specs=[anywhere] * 5 + [scalars] * 2,
        out_specs=anywhere,
        scratch_shapes=[
            pltpu.VMEM((MOST_TILES * TILE_TOKENS, HEADS * HEAD_WIDTH), half),
            pltpu.VMEM((2, 2, 1024, HEAD_WIDTH), half),
            pltpu.VMEM((2, 2, MOST_TILES * TILE_TOKENS, HEAD_WIDTH), half),
            pltpu.VMEM(four, half),
            pltpu.VMEM(pair, half),
            pltpu.VMEM(pair, half),
            pltpu.VMEM(pair, half),
            pltpu.VMEM(pair, half),
            pltpu.VMEM(four, half),
            dma((5,)),
            dma((2, 2)),
            dma((2, 2, 3)),
            dma((2, 2, 3)),
            dma((2, 2)),
            dma((2, 2)),
            dma((2, 2)),
            dma((2, 2)),
            dma((HEADS,)),
            dma((HEADS,)),
            dma((HEADS,)),
            dma((HEADS,)),
            dma((HEADS,)),
        ],
        compiler_params=pltpu.CompilerParams(
            collective_id=0, has_side_effects=True, vmem_limit_bytes=56 << 20
        ),
    )(
        queries[0], prompt_keys[0], prompt_value_rows[0], reply_keys[0], response_values[0],
        lengths, jnp.swapaxes(hand_counts, 1, 2),
    )
    return out.reshape(1, MOST_TILES * TILE_TOKENS, -1)


def solution(mesh):
    placed = (
        P("prompt", "sample", None),
        P("prompt", "sample", None),
        P("prompt", "sample", None),
        P("prompt", "sample", None),
        P("prompt", "sample", None),
        P("prompt", None),
        P("prompt", None, None),
    )
    return jax.shard_map(
        per_device,
        mesh=mesh,
        in_specs=placed,
        out_specs=P("prompt", "sample", None),
        check_vma=False,
    )
```

```python
import functools
import math

import jax
import jax.numpy as jnp
from jax import lax
from jax.experimental import pallas as pl
from jax.experimental.pallas import tpu as pltpu
from jax.sharding import PartitionSpec as P

KEY_VALUE_HEADS = 2
QUERY_PER_KEY = 7
HEADS = KEY_VALUE_HEADS * QUERY_PER_KEY
HEAD_WIDTH = 128
TILE_TOKENS = 128
MOST_TILES = 4
ALONG_X = 4
ALONG_Z = 4
LAG_SECOND = 3
LAG_OUT = 6
PARTS = 1
EARLY_FROM = 4
EARLY = 1

LOG_SCALE = math.log2(math.e) / math.sqrt(HEAD_WIDTH)


def dot_nt(a, b):
    return lax.dot_general(a, b, (((1,), (1,)), ((), ())), preferred_element_type=jnp.float32)


def softmax_parts(scores):
    top = jnp.max(scores, axis=-1, keepdims=True)
    weights = jnp.exp2((scores - top) * LOG_SCALE)
    total = jnp.sum(weights, axis=-1, keepdims=True)
    return top, weights.astype(jnp.bfloat16), total


def weigh(weights, values):
    return jnp.dot(weights, values, preferred_element_type=jnp.float32)


def reply_part(query, keys, values, half):
    rows = 2 * TILE_TOKENS
    seen = (half + 1) * rows
    scores = dot_nt(query, keys[:seen])
    row = lax.broadcasted_iota(jnp.int32, (rows, rows), 0)
    col = lax.broadcasted_iota(jnp.int32, (rows, rows), 1)
    last = jnp.where(col <= row, scores[:, half * rows :], -1e30)
    if half:
        last = jnp.concatenate([scores[:, : half * rows], last], axis=1)
    top, weights, total = softmax_parts(last)
    return top, total, weigh(weights, values[:seen])


def combine_level(p_top, p_total, p_mix, r_level, r_mix):
    p_level = p_top * LOG_SCALE
    top = jnp.maximum(p_level, r_level)
    a = jnp.exp2(p_level - top)
    b = jnp.exp2(r_level - top)
    inverse = 1.0 / (a * p_total + b)
    return (p_mix * (a * inverse) + r_mix.astype(jnp.float32) * (b * inverse)).astype(jnp.bfloat16)


def combine(p_top, p_total, p_mix, r_top, r_total, r_mix):
    top = jnp.maximum(p_top, r_top)
    a = jnp.exp2((p_top - top) * LOG_SCALE)
    b = jnp.exp2((r_top - top) * LOG_SCALE)
    inverse = 1.0 / (a * p_total + b * r_total)
    return (p_mix * (a * inverse) + r_mix * (b * inverse)).astype(jnp.bfloat16)


def kernel(
    q_hbm, pk_hbm, pv_hbm, rk_hbm, rv_hbm, len_ref, hand_ref, out_hbm,
    q_buf, kv, rkv, own, send1, recv1, send2, recv2, out_buf,
    e_send, e_recv, l_send, l_recv,
    in_sem, own_sem, z_send, z_recv, x_send, x_recv,
    s1_sem, r1_sem, s2_sem, r2_sem, out_sem, es_sem, er_sem,
):
    me = lax.axis_index("sample")
    z = me // ALONG_X
    x = me % ALONG_X

    def at(zz, xx):
        return {"sample": zz * ALONG_X + xx}

    depths = [z, z + 1 - 2 * (z % 2), (z + 2) % ALONG_Z, ALONG_Z - 1 - z]
    z_peers = [at(depth, x) for depth in depths[1:]]
    across = at(z, (x + 2) % ALONG_X)
    right = at(z, (x + 1) % ALONG_X)
    left = at(z, (x + 3) % ALONG_X)
    first_partner = z_peers[1]
    second_partner = z_peers[0]
    MESH = pl.DeviceIdType.MESH

    barrier = pltpu.get_barrier_semaphore()
    for peer in z_peers + [right, left, across]:
        pl.semaphore_signal(barrier, inc=1, device_id=peer, device_id_type=MESH)

    width = HEAD_WIDTH
    own_rows = pl.ds(pl.multiple_of(x * 256 + z * 64, 64), 64)
    prompt_side = (pk_hbm, pv_hbm)
    reply_side = (rk_hbm, rv_hbm)
    own_copies = [
        pltpu.make_async_copy(
            prompt_side[kind].at[:, g * width : (g + 1) * width],
            kv.at[g, kind, own_rows, :],
            own_sem.at[g, kind],
        )
        for g in range(2)
        for kind in range(2)
    ]
    in_copies = [pltpu.make_async_copy(q_hbm, q_buf, in_sem.at[0])] + [
        pltpu.make_async_copy(
            reply_side[kind].at[:, g * width : (g + 1) * width],
            rkv.at[g, kind],
            in_sem.at[1 + 2 * g + kind],
        )
        for g in range(2)
        for kind in range(2)
    ]
    for copy in own_copies + in_copies:
        copy.start()

    first_index = depths[2] * ALONG_X + x
    second_index = depths[1] * ALONG_X + x
    give1 = hand_ref[0, 0, me]
    get1 = hand_ref[0, 0, first_index]
    give2 = hand_ref[0, 1, me]
    get2 = hand_ref[0, 1, second_index]
    keep1 = len_ref[0, me] - give1
    keep2 = keep1 + get1 - give2
    load2 = keep2 + get2

    def block_rows(zz, xx):
        return pl.ds(pl.multiple_of(xx * 256 + zz * 64, 64), 64)

    def z_copy(g, i):
        own_block = kv.at[g, :, own_rows, :]
        return pltpu.make_async_remote_copy(
            own_block, own_block, z_send.at[g, i - 1], z_recv.at[g, i - 1],
            device_id=z_peers[i - 1], device_id_type=MESH,
        )

    def x_copy(g, i, way):
        block = kv.at[g, :, block_rows(depths[i], x), :]
        return pltpu.make_async_remote_copy(
            block, block, x_send.at[g, i, way], x_recv.at[g, i, way],
            device_id=(right, left, across)[way], device_id_type=MESH,
        )

    def forward_x(g, i):
        for way in range(3):
            x_copy(g, i, way).start()

    def gathered(g):
        for i in range(ALONG_Z):
            for way in range(3):
                x_copy(g, i, way).wait_recv()

    def top_two(keep, one, two, three):
        first = jnp.where(keep == 1, one, jnp.where(keep == 2, two, three))
        return first, jnp.where(keep == 1, two, three)

    early_copies = [
        pltpu.make_async_remote_copy(
            e_send, e_recv, es_sem.at[0], er_sem.at[0],
            device_id=first_partner, device_id_type=MESH,
        ),
        pltpu.make_async_remote_copy(
            l_send, l_recv, es_sem.at[1], er_sem.at[1],
            device_id=first_partner, device_id_type=MESH,
        ),
    ]

    for copy in own_copies:
        copy.wait()
    pl.semaphore_wait(barrier, 6)
    for i in (3, 1, 2):
        z_copy(0, i).start()
    forward_x(0, 0)

    for copy in in_copies:
        copy.wait()
    lane = lax.broadcasted_iota(jnp.int32, (TILE_TOKENS, width), 1)
    levels = jnp.zeros((TILE_TOKENS, width), jnp.float32)
    for e in range(EARLY):
        c = EARLY_FROM + e
        g = c // QUERY_PER_KEY
        mixes, sums = [], []
        for h in range(2):
            rows = slice(2 * h * TILE_TOKENS, 2 * (h + 1) * TILE_TOKENS)
            cols = slice(c * width, (c + 1) * width)
            top, total, mix = reply_part(q_buf[rows, cols], rkv.at[g, 0], rkv.at[g, 1], h)
            mix = (mix * (1.0 / total)).astype(jnp.bfloat16)
            level = top * LOG_SCALE + jnp.log2(total)
            mixes += [mix[:TILE_TOKENS], mix[TILE_TOKENS:]]
            sums += [level[:TILE_TOKENS], level[TILE_TOKENS:]]
        ask = [
            q_buf[t * TILE_TOKENS : (t + 1) * TILE_TOKENS, c * width : (c + 1) * width]
            for t in range(MOST_TILES)
        ]
        for kind, tiles in enumerate((ask, mixes)):
            for j, tile in enumerate(top_two(keep1, *tiles[1:])):
                e_send[e, kind, j * TILE_TOKENS : (j + 1) * TILE_TOKENS] = tile
        for j, level in enumerate(top_two(keep1, *sums[1:])):
            levels = jnp.where(lane == 2 * e + j, level, levels)
    l_send[...] = levels.T[:8]

    for copy in early_copies:
        copy.start()
    for i in (1, 2, 3):
        z_copy(1, i).start()
    for i in (1, 3, 2):
        z_copy(0, i).wait_recv()
        forward_x(0, i)

    height = TILE_TOKENS // PARTS

    def rows_of(part):
        return slice(part * height, (part + 1) * height)

    def s1_copy(c, part):
        return pltpu.make_async_remote_copy(
            send1.at[c, :, rows_of(part), :], recv1.at[c, :, rows_of(part), :],
            s1_sem.at[c, part], r1_sem.at[c, part],
            device_id=first_partner, device_id_type=MESH,
        )

    def s2_copy(c, part):
        return pltpu.make_async_remote_copy(
            send2.at[c, :, rows_of(part), :], recv2.at[c, :, rows_of(part), :],
            s2_sem.at[c, part], r2_sem.at[c, part],
            device_id=second_partner, device_id_type=MESH,
        )

    def out_copy(c):
        return pltpu.make_async_copy(
            out_buf.at[c],
            out_hbm.at[:, :, pl.ds(pl.multiple_of(c * width, width), width)],
            out_sem.at[c],
        )

    def placed(keep, one, two, three, a, b):
        return (
            jnp.where(keep == 1, a, one),
            jnp.where(keep == 1, b, jnp.where(keep == 2, a, two)),
            jnp.where(keep == 2, b, jnp.where(keep == 3, a, three)),
        )

    def attend(c):
        g = c // QUERY_PER_KEY
        cols = pl.ds(pl.multiple_of(c * width, width), width)
        rows = 2 * TILE_TOKENS
        reply = [
            reply_part(q_buf[h * rows : (h + 1) * rows, cols], rkv.at[g, 0], rkv.at[g, 1], h)
            for h in range(2)
        ]

        @pl.when(c == 0)
        def _():
            gathered(0)

        @pl.when(c == QUERY_PER_KEY)
        def _():
            gathered(1)

        tiles = []
        for h in range(2):
            scores = dot_nt(q_buf[h * rows : (h + 1) * rows, cols], kv[g, 0])
            top, weights, total = softmax_parts(scores)
            mix = weigh(weights, kv[g, 1])
            r_top, r_total, r_mix = reply[h]
            result = combine(top, total, mix, r_top, r_total, r_mix)
            tiles += [result[:TILE_TOKENS], result[TILE_TOKENS:]]
        for t in range(MOST_TILES):
            own[c, t] = tiles[t]
        first, second = top_two(keep1, tiles[1], tiles[2], tiles[3])
        send1[c, 0] = first
        send1[c, 1] = second

    def arrived(e):
        c = EARLY_FROM + e
        g = c // QUERY_PER_KEY
        scores = dot_nt(e_recv[e, 0], kv[g, 0])
        top, weights, total = softmax_parts(scores)
        mix = weigh(weights, kv[g, 1])
        spread = jnp.concatenate(
            [l_recv[...], jnp.zeros((TILE_TOKENS - 8, width), jnp.float32)], axis=0
        ).T
        level = jnp.concatenate([spread[:, 2 * e : 2 * e + 1], spread[:, 2 * e + 1 : 2 * e + 2]], axis=0)
        result = combine_level(top, total, mix, level, e_recv[e, 1])
        recv1[c, 0] = result[:TILE_TOKENS]
        recv1[c, 1] = result[TILE_TOKENS:]

    def step(c, _):
        @pl.when(c < HEADS)
        def _():
            attend(c)

        late = (c < EARLY_FROM) | (c >= EARLY_FROM + EARLY)

        @pl.when((c < HEADS) & late)
        def _():
            for part in range(PARTS):
                s1_copy(c, part).start()

        @pl.when(c == EARLY_FROM)
        def _():
            for copy in early_copies:
                copy.wait_recv()

        for e in range(EARLY):
            @pl.when(c == EARLY_FROM + e)
            def _():
                arrived(e)

        @pl.when(c == 0)
        def _():
            for i in (1, 2, 3):
                z_copy(1, i).wait_recv()
            for i in range(ALONG_Z):
                forward_x(1, i)

        @pl.when((c >= LAG_SECOND) & (c < HEADS + LAG_SECOND))
        def _():
            d = c - LAG_SECOND
            waits = (d < EARLY_FROM) | (d >= EARLY_FROM + EARLY)
            for part in range(PARTS):
                r = rows_of(part)

                @pl.when(waits)
                def _():
                    s1_copy(d, part).wait_recv()

                mine = [own[d, t, r] for t in (1, 2, 3)]
                slots = placed(keep1, *mine, recv1[d, 0, r], recv1[d, 1, r])
                first, second = top_two(keep2, *slots)
                send2[d, 0, r] = first
                send2[d, 1, r] = second
                s2_copy(d, part).start()
                for t in range(3):
                    own[d, t + 1, r] = slots[t]

        @pl.when(c >= LAG_OUT)
        def _():
            e = c - LAG_OUT
            for part in range(PARTS):
                s2_copy(e, part).wait_recv()
            slots = placed(keep2, own[e, 1], own[e, 2], own[e, 3], recv2[e, 0], recv2[e, 1])
            out_buf[e, 0] = own[e, 0]
            for t in range(3):
                out_buf[e, t + 1] = jnp.where(t + 1 < load2, slots[t], jnp.zeros_like(slots[t]))
            out_copy(e).start()

        return 0

    lax.fori_loop(0, HEADS + LAG_OUT, step, 0)

    for g in range(2):
        for i in (1, 2, 3):
            z_copy(g, i).wait_send()
        for i in range(ALONG_Z):
            for way in range(3):
                x_copy(g, i, way).wait_send()

    for copy in early_copies:
        copy.wait_send()

    def finish(c, _):
        @pl.when((c < EARLY_FROM) | (c >= EARLY_FROM + EARLY))
        def _():
            for part in range(PARTS):
                s1_copy(c, part).wait_send()

        for part in range(PARTS):
            s2_copy(c, part).wait_send()
        out_copy(c).wait()
        return 0

    lax.fori_loop(0, HEADS, finish, 0)


def per_device(
    queries, prompt_keys, prompt_value_rows, reply_keys, response_values, lengths, hand_counts
):
    half = jnp.bfloat16
    pair = (HEADS, 2, TILE_TOKENS, HEAD_WIDTH)
    four = (HEADS, MOST_TILES, TILE_TOKENS, HEAD_WIDTH)
    dma = pltpu.SemaphoreType.DMA
    anywhere = pl.BlockSpec(memory_space=pl.ANY)
    scalars = pl.BlockSpec(memory_space=pltpu.SMEM)
    out = pl.pallas_call(
        kernel,
        out_shape=pltpu.VMEM((MOST_TILES, TILE_TOKENS, HEADS * HEAD_WIDTH), half),
        in_specs=[anywhere] * 5 + [scalars] * 2,
        out_specs=anywhere,
        scratch_shapes=[
            pltpu.VMEM((MOST_TILES * TILE_TOKENS, HEADS * HEAD_WIDTH), half),
            pltpu.VMEM((2, 2, 1024, HEAD_WIDTH), half),
            pltpu.VMEM((2, 2, MOST_TILES * TILE_TOKENS, HEAD_WIDTH), half),
            pltpu.VMEM(four, half),
            pltpu.VMEM(pair, half),
            pltpu.VMEM(pair, half),
            pltpu.VMEM(pair, half),
            pltpu.VMEM(pair, half),
            pltpu.VMEM(four, half),
            pltpu.VMEM((EARLY, 2, 2 * TILE_TOKENS, HEAD_WIDTH), half),
            pltpu.VMEM((EARLY, 2, 2 * TILE_TOKENS, HEAD_WIDTH), half),
            pltpu.VMEM((8, HEAD_WIDTH), jnp.float32),
            pltpu.VMEM((8, HEAD_WIDTH), jnp.float32),
            dma((5,)),
            dma((2, 2)),
            dma((2, 3)),
            dma((2, 3)),
            dma((2, ALONG_Z, 3)),
            dma((2, ALONG_Z, 3)),
            dma((HEADS, PARTS)),
            dma((HEADS, PARTS)),
            dma((HEADS, PARTS)),
            dma((HEADS, PARTS)),
            dma((HEADS,)),
            dma((2,)),
            dma((2,)),
        ],
        compiler_params=pltpu.CompilerParams(
            collective_id=0, has_side_effects=True, vmem_limit_bytes=56 << 20
        ),
    )(
        queries[0], prompt_keys[0], prompt_value_rows[0], reply_keys[0], response_values[0],
        lengths, jnp.swapaxes(hand_counts, 1, 2),
    )
    return out.reshape(1, MOST_TILES * TILE_TOKENS, -1)


def solution(mesh):
    placed = (
        P("prompt", "sample", None),
        P("prompt", "sample", None),
        P("prompt", "sample", None),
        P("prompt", "sample", None),
        P("prompt", "sample", None),
        P("prompt", None),
        P("prompt", None, None),
    )
    return jax.shard_map(
        per_device,
        mesh=mesh,
        in_specs=placed,
        out_specs=P("prompt", "sample", None),
        check_vma=False,
    )
```

```python
import functools
import math

import jax
import jax.numpy as jnp
from jax import lax
from jax.experimental import pallas as pl
from jax.experimental.pallas import tpu as pltpu
from jax.sharding import PartitionSpec as P

KEY_VALUE_HEADS = 2
QUERY_PER_KEY = 7
HEADS = KEY_VALUE_HEADS * QUERY_PER_KEY
HEAD_WIDTH = 128
TILE_TOKENS = 128
MOST_TILES = 4
ALONG_X = 4
ALONG_Z = 4
LAG_SECOND = 3
LAG_OUT = 6
PARTS = 1
EARLY_FROM = 4
EARLY = 1

LOG_SCALE = math.log2(math.e) / math.sqrt(HEAD_WIDTH)


def dot_nt(a, b):
    return lax.dot_general(a, b, (((1,), (1,)), ((), ())), preferred_element_type=jnp.float32)


def softmax_parts(scores):
    top = jnp.max(scores, axis=-1, keepdims=True)
    weights = jnp.exp2((scores - top) * LOG_SCALE)
    total = jnp.sum(weights, axis=-1, keepdims=True)
    return top, weights.astype(jnp.bfloat16), total


def weigh(weights, values):
    return jnp.dot(weights, values, preferred_element_type=jnp.float32)


def reply_part(query, keys, values, half):
    rows = 2 * TILE_TOKENS
    seen = (half + 1) * rows
    scores = dot_nt(query, keys[:seen])
    row = lax.broadcasted_iota(jnp.int32, (rows, rows), 0)
    col = lax.broadcasted_iota(jnp.int32, (rows, rows), 1)
    last = jnp.where(col <= row, scores[:, half * rows :], -1e30)
    if half:
        last = jnp.concatenate([scores[:, : half * rows], last], axis=1)
    top, weights, total = softmax_parts(last)
    return top, total, weigh(weights, values[:seen])


def combine_level(p_top, p_total, p_mix, r_level, r_mix):
    p_level = p_top * LOG_SCALE
    top = jnp.maximum(p_level, r_level)
    a = jnp.exp2(p_level - top)
    b = jnp.exp2(r_level - top)
    inverse = 1.0 / (a * p_total + b)
    return (p_mix * (a * inverse) + r_mix.astype(jnp.float32) * (b * inverse)).astype(jnp.bfloat16)


def joint_part(query, p_keys, p_values, r_keys, r_values, half):
    rows = 2 * TILE_TOKENS
    seen = (half + 1) * rows
    scores = dot_nt(query, r_keys[:seen])
    row = lax.broadcasted_iota(jnp.int32, (rows, rows), 0)
    col = lax.broadcasted_iota(jnp.int32, (rows, rows), 1)
    pieces = [jnp.where(col <= row, scores[:, half * rows :], -1e30)]
    values = [r_values[half * rows : seen]]
    if half:
        pieces.append(scores[:, :rows])
        values.append(r_values[:rows])
    pieces.append(dot_nt(query, p_keys))
    values.append(p_values)
    top = functools.reduce(
        jnp.maximum, [jnp.max(piece, axis=-1, keepdims=True) for piece in pieces]
    )
    total, mix = 0.0, 0.0
    for piece, value in zip(pieces, values):
        weights = jnp.exp2((piece - top) * LOG_SCALE)
        total = total + jnp.sum(weights, axis=-1, keepdims=True)
        mix = mix + weigh(weights.astype(jnp.bfloat16), value)
    return (mix * (1.0 / total)).astype(jnp.bfloat16)


def kernel(
    q_hbm, pk_hbm, pv_hbm, rk_hbm, rv_hbm, len_ref, hand_ref, out_hbm,
    q_buf, kv, rkv, own, send1, recv1, send2, recv2, out_buf,
    e_send, e_recv, l_send, l_recv,
    in_sem, own_sem, z_send, z_recv, x_send, x_recv,
    s1_sem, r1_sem, s2_sem, r2_sem, out_sem, es_sem, er_sem,
):
    me = lax.axis_index("sample")
    z = me // ALONG_X
    x = me % ALONG_X

    def at(zz, xx):
        return {"sample": zz * ALONG_X + xx}

    depths = [z, z + 1 - 2 * (z % 2), (z + 2) % ALONG_Z, ALONG_Z - 1 - z]
    z_peers = [at(depth, x) for depth in depths[1:]]
    across = at(z, (x + 2) % ALONG_X)
    right = at(z, (x + 1) % ALONG_X)
    left = at(z, (x + 3) % ALONG_X)
    first_partner = z_peers[1]
    second_partner = z_peers[0]
    MESH = pl.DeviceIdType.MESH

    barrier = pltpu.get_barrier_semaphore()
    for peer in z_peers + [right, left, across]:
        pl.semaphore_signal(barrier, inc=1, device_id=peer, device_id_type=MESH)

    width = HEAD_WIDTH
    own_rows = pl.ds(pl.multiple_of(x * 256 + z * 64, 64), 64)
    prompt_side = (pk_hbm, pv_hbm)
    reply_side = (rk_hbm, rv_hbm)
    own_copies = [
        pltpu.make_async_copy(
            prompt_side[kind].at[:, g * width : (g + 1) * width],
            kv.at[g, kind, own_rows, :],
            own_sem.at[g, kind],
        )
        for g in range(2)
        for kind in range(2)
    ]
    in_copies = [pltpu.make_async_copy(q_hbm, q_buf, in_sem.at[0])] + [
        pltpu.make_async_copy(
            reply_side[kind].at[:, g * width : (g + 1) * width],
            rkv.at[g, kind],
            in_sem.at[1 + 2 * g + kind],
        )
        for g in range(2)
        for kind in range(2)
    ]
    for copy in own_copies + in_copies:
        copy.start()

    first_index = depths[2] * ALONG_X + x
    second_index = depths[1] * ALONG_X + x
    give1 = hand_ref[0, 0, me]
    get1 = hand_ref[0, 0, first_index]
    give2 = hand_ref[0, 1, me]
    get2 = hand_ref[0, 1, second_index]
    keep1 = len_ref[0, me] - give1
    keep2 = keep1 + get1 - give2
    load2 = keep2 + get2

    def block_rows(zz, xx):
        return pl.ds(pl.multiple_of(xx * 256 + zz * 64, 64), 64)

    def z_copy(g, i):
        block = kv.at[g, :, block_rows(depths[2 if i == 3 else 0], x), :]
        return pltpu.make_async_remote_copy(
            block, block, z_send.at[g, i - 1], z_recv.at[g, i - 1],
            device_id=z_peers[0 if i == 3 else i - 1], device_id_type=MESH,
        )

    def x_copy(g, i, way):
        block = kv.at[g, :, block_rows(depths[i], x), :]
        return pltpu.make_async_remote_copy(
            block, block, x_send.at[g, i, way], x_recv.at[g, i, way],
            device_id=(right, left, across)[way], device_id_type=MESH,
        )

    def forward_x(g, i):
        for way in (2, 0, 1):
            x_copy(g, i, way).start()

    def gathered(g):
        for i in range(ALONG_Z):
            for way in range(3):
                x_copy(g, i, way).wait_recv()

    def top_two(keep, one, two, three):
        first = jnp.where(keep == 1, one, jnp.where(keep == 2, two, three))
        return first, jnp.where(keep == 1, two, three)

    early_copies = [
        pltpu.make_async_remote_copy(
            e_send, e_recv, es_sem.at[0], er_sem.at[0],
            device_id=first_partner, device_id_type=MESH,
        ),
        pltpu.make_async_remote_copy(
            l_send, l_recv, es_sem.at[1], er_sem.at[1],
            device_id=first_partner, device_id_type=MESH,
        ),
    ]

    for copy in own_copies:
        copy.wait()
    pl.semaphore_wait(barrier, 6)
    for i in (2, 1):
        z_copy(0, i).start()
    forward_x(0, 0)

    for copy in in_copies:
        copy.wait()
    lane = lax.broadcasted_iota(jnp.int32, (TILE_TOKENS, width), 1)
    levels = jnp.zeros((TILE_TOKENS, width), jnp.float32)
    for e in range(EARLY):
        c = EARLY_FROM + e
        g = c // QUERY_PER_KEY
        mixes, sums = [], []
        for h in range(2):
            rows = slice(2 * h * TILE_TOKENS, 2 * (h + 1) * TILE_TOKENS)
            cols = slice(c * width, (c + 1) * width)
            top, total, mix = reply_part(q_buf[rows, cols], rkv.at[g, 0], rkv.at[g, 1], h)
            mix = (mix * (1.0 / total)).astype(jnp.bfloat16)
            level = top * LOG_SCALE + jnp.log2(total)
            mixes += [mix[:TILE_TOKENS], mix[TILE_TOKENS:]]
            sums += [level[:TILE_TOKENS], level[TILE_TOKENS:]]
        ask = [
            q_buf[t * TILE_TOKENS : (t + 1) * TILE_TOKENS, c * width : (c + 1) * width]
            for t in range(MOST_TILES)
        ]
        for kind, tiles in enumerate((ask, mixes)):
            for j, tile in enumerate(top_two(keep1, *tiles[1:])):
                e_send[e, kind, j * TILE_TOKENS : (j + 1) * TILE_TOKENS] = tile
        for j, level in enumerate(top_two(keep1, *sums[1:])):
            levels = jnp.where(lane == 2 * e + j, level, levels)
    l_send[...] = levels.T[:8]

    z_copy(0, 1).wait_recv()
    forward_x(0, 1)
    z_copy(0, 2).wait_recv()
    z_copy(0, 3).start()
    forward_x(0, 2)
    for copy in early_copies:
        copy.start()
    for i in (2, 1):
        z_copy(1, i).start()
    z_copy(0, 3).wait_recv()
    forward_x(0, 3)

    height = TILE_TOKENS // PARTS

    def rows_of(part):
        return slice(part * height, (part + 1) * height)

    def s1_copy(c, part):
        return pltpu.make_async_remote_copy(
            send1.at[c, :, rows_of(part), :], recv1.at[c, :, rows_of(part), :],
            s1_sem.at[c, part], r1_sem.at[c, part],
            device_id=first_partner, device_id_type=MESH,
        )

    def s2_copy(c, part):
        return pltpu.make_async_remote_copy(
            send2.at[c, :, rows_of(part), :], recv2.at[c, :, rows_of(part), :],
            s2_sem.at[c, part], r2_sem.at[c, part],
            device_id=second_partner, device_id_type=MESH,
        )

    def out_copy(c):
        return pltpu.make_async_copy(
            out_buf.at[c],
            out_hbm.at[:, :, pl.ds(pl.multiple_of(c * width, width), width)],
            out_sem.at[c],
        )

    def placed(keep, one, two, three, a, b):
        return (
            jnp.where(keep == 1, a, one),
            jnp.where(keep == 1, b, jnp.where(keep == 2, a, two)),
            jnp.where(keep == 2, b, jnp.where(keep == 3, a, three)),
        )

    def attend(c):
        g = c // QUERY_PER_KEY
        cols = pl.ds(pl.multiple_of(c * width, width), width)
        rows = 2 * TILE_TOKENS
        tiles = []
        for h in range(2):
            result = joint_part(
                q_buf[h * rows : (h + 1) * rows, cols],
                kv[g, 0], kv[g, 1], rkv.at[g, 0], rkv.at[g, 1], h,
            )
            tiles += [result[:TILE_TOKENS], result[TILE_TOKENS:]]
        for t in range(MOST_TILES):
            own[c, t] = tiles[t]
        first, second = top_two(keep1, tiles[1], tiles[2], tiles[3])
        send1[c, 0] = first
        send1[c, 1] = second

    def arrived(e):
        c = EARLY_FROM + e
        g = c // QUERY_PER_KEY
        scores = dot_nt(e_recv[e, 0], kv[g, 0])
        top, weights, total = softmax_parts(scores)
        mix = weigh(weights, kv[g, 1])
        spread = jnp.concatenate(
            [l_recv[...], jnp.zeros((TILE_TOKENS - 8, width), jnp.float32)], axis=0
        ).T
        level = jnp.concatenate([spread[:, 2 * e : 2 * e + 1], spread[:, 2 * e + 1 : 2 * e + 2]], axis=0)
        result = combine_level(top, total, mix, level, e_recv[e, 1])
        recv1[c, 0] = result[:TILE_TOKENS]
        recv1[c, 1] = result[TILE_TOKENS:]

    def step(c, _):
        @pl.when(c == 0)
        def _():
            gathered(0)

        @pl.when(c == QUERY_PER_KEY)
        def _():
            gathered(1)

        @pl.when(c < HEADS)
        def _():
            attend(c)

        late = (c < EARLY_FROM) | (c >= EARLY_FROM + EARLY)

        @pl.when((c < HEADS) & late)
        def _():
            for part in range(PARTS):
                s1_copy(c, part).start()

        @pl.when(c == EARLY_FROM)
        def _():
            for copy in early_copies:
                copy.wait_recv()

        for e in range(EARLY):
            @pl.when(c == EARLY_FROM + e)
            def _():
                arrived(e)

        @pl.when(c == 0)
        def _():
            for i in (1, 2):
                z_copy(1, i).wait_recv()
            z_copy(1, 3).start()
            for i in range(3):
                forward_x(1, i)

        @pl.when(c == 2)
        def _():
            z_copy(1, 3).wait_recv()
            forward_x(1, 3)

        @pl.when((c >= LAG_SECOND) & (c < HEADS + LAG_SECOND))
        def _():
            d = c - LAG_SECOND
            waits = (d < EARLY_FROM) | (d >= EARLY_FROM + EARLY)
            for part in range(PARTS):
                r = rows_of(part)

                @pl.when(waits)
                def _():
                    s1_copy(d, part).wait_recv()

                mine = [own[d, t, r] for t in (1, 2, 3)]
                slots = placed(keep1, *mine, recv1[d, 0, r], recv1[d, 1, r])
                first, second = top_two(keep2, *slots)
                send2[d, 0, r] = first
                send2[d, 1, r] = second
                s2_copy(d, part).start()
                for t in range(3):
                    own[d, t + 1, r] = slots[t]

        @pl.when(c >= LAG_OUT)
        def _():
            e = c - LAG_OUT
            for part in range(PARTS):
                s2_copy(e, part).wait_recv()
            slots = placed(keep2, own[e, 1], own[e, 2], own[e, 3], recv2[e, 0], recv2[e, 1])
            out_buf[e, 0] = own[e, 0]
            for t in range(3):
                out_buf[e, t + 1] = jnp.where(t + 1 < load2, slots[t], jnp.zeros_like(slots[t]))
            out_copy(e).start()

        return 0

    lax.fori_loop(0, HEADS + LAG_OUT, step, 0)

    for g in range(2):
        for i in (1, 2, 3):
            z_copy(g, i).wait_send()
        for i in range(ALONG_Z):
            for way in range(3):
                x_copy(g, i, way).wait_send()

    for copy in early_copies:
        copy.wait_send()

    def finish(c, _):
        @pl.when((c < EARLY_FROM) | (c >= EARLY_FROM + EARLY))
        def _():
            for part in range(PARTS):
                s1_copy(c, part).wait_send()

        for part in range(PARTS):
            s2_copy(c, part).wait_send()
        out_copy(c).wait()
        return 0

    lax.fori_loop(0, HEADS, finish, 0)


def per_device(
    queries, prompt_keys, prompt_value_rows, reply_keys, response_values, lengths, hand_counts
):
    half = jnp.bfloat16
    pair = (HEADS, 2, TILE_TOKENS, HEAD_WIDTH)
    four = (HEADS, MOST_TILES, TILE_TOKENS, HEAD_WIDTH)
    dma = pltpu.SemaphoreType.DMA
    anywhere = pl.BlockSpec(memory_space=pl.ANY)
    scalars = pl.BlockSpec(memory_space=pltpu.SMEM)
    out = pl.pallas_call(
        kernel,
        out_shape=pltpu.VMEM((MOST_TILES, TILE_TOKENS, HEADS * HEAD_WIDTH), half),
        in_specs=[anywhere] * 5 + [scalars] * 2,
        out_specs=anywhere,
        scratch_shapes=[
            pltpu.VMEM((MOST_TILES * TILE_TOKENS, HEADS * HEAD_WIDTH), half),
            pltpu.VMEM((2, 2, 1024, HEAD_WIDTH), half),
            pltpu.VMEM((2, 2, MOST_TILES * TILE_TOKENS, HEAD_WIDTH), half),
            pltpu.VMEM(four, half),
            pltpu.VMEM(pair, half),
            pltpu.VMEM(pair, half),
            pltpu.VMEM(pair, half),
            pltpu.VMEM(pair, half),
            pltpu.VMEM(four, half),
            pltpu.VMEM((EARLY, 2, 2 * TILE_TOKENS, HEAD_WIDTH), half),
            pltpu.VMEM((EARLY, 2, 2 * TILE_TOKENS, HEAD_WIDTH), half),
            pltpu.VMEM((8, HEAD_WIDTH), jnp.float32),
            pltpu.VMEM((8, HEAD_WIDTH), jnp.float32),
            dma((5,)),
            dma((2, 2)),
            dma((2, 3)),
            dma((2, 3)),
            dma((2, ALONG_Z, 3)),
            dma((2, ALONG_Z, 3)),
            dma((HEADS, PARTS)),
            dma((HEADS, PARTS)),
            dma((HEADS, PARTS)),
            dma((HEADS, PARTS)),
            dma((HEADS,)),
            dma((2,)),
            dma((2,)),
        ],
        compiler_params=pltpu.CompilerParams(
            collective_id=0, has_side_effects=True, vmem_limit_bytes=56 << 20
        ),
    )(
        queries[0], prompt_keys[0], prompt_value_rows[0], reply_keys[0], response_values[0],
        lengths, jnp.swapaxes(hand_counts, 1, 2),
    )
    return out.reshape(1, MOST_TILES * TILE_TOKENS, -1)


def solution(mesh):
    placed = (
        P("prompt", "sample", None),
        P("prompt", "sample", None),
        P("prompt", "sample", None),
        P("prompt", "sample", None),
        P("prompt", "sample", None),
        P("prompt", None),
        P("prompt", None, None),
    )
    return jax.shard_map(
        per_device,
        mesh=mesh,
        in_specs=placed,
        out_specs=P("prompt", "sample", None),
        check_vma=False,
    )
```
